32 devices in a mesh: replica: 4 (over y, core), kvhead: 4 (over z), ffn: 2 (over x).
Axes of the slice: x: 2, y: 2, z: 4, core: 2. Of those that a mesh axis runs over, the one named last changes fastest.
Arguments:
- queries: bfloat16 [16, 16384], P('replica', 'kvhead'), may hold values from -400 to 400
- k_cache: bfloat16 [512, 64, 1024], P(('replica', 'ffn'), None, 'kvhead'), may hold values from -6 to 6
- v_cache: bfloat16 [512, 64, 1024], P(('replica', 'ffn'), None, 'kvhead'), may hold values from -6 to 6
- page_table: int32 [16, 32], P('replica', 'ffn'), may hold values from 0 to 63, as said below
- seq_lens: int32 [16], P('replica'), may hold values from 1 to 2048, as said below
- out_proj: bfloat16 [16384, 16384], P('kvhead', ('replica', 'ffn')), may hold values from -0.125 to 0.125
- residual: bfloat16 [16, 16384], P('kvhead', ('replica', 'ffn')), may hold values from -40 to 40
- norm_gain: bfloat16 [16384], P(('replica', 'ffn')), may hold values from 0.099609375 to 1.8984375
- gate_weight: bfloat16 [26624, 16384], P(('replica', 'kvhead', 'ffn')), may hold values from -0.046875 to 0.046875
- up_weight: bfloat16 [26624, 16384], P(('replica', 'kvhead', 'ffn')), may hold values from -0.046875 to 0.046875
Outputs:
- post_attn: bfloat16 [16, 16384], P('kvhead', ('replica', 'ffn'))
- hidden: bfloat16 [16, 26624], P(None, ('replica', 'kvhead', 'ffn'))
The draws below stay inside these ranges and needn't reach their ends.
Inputs may be any that keep to these rules, and one draw needn't show every extreme that they name: `page_table`: over the 4 rows of one replica, the entries of page columns j with the same j // 16 name every pool page 0 to 63 exactly once. `seq_lens`: some row has length 2048.
All inputs are finite; a program needn't handle non-finite values.
Results may differ from the reference program's by a relative error of at most 0.0079.
Values may be sent and summed in bfloat16 or wider, within the bound.
A program may use at most 192 MiB of HBM per device.

```python
import math
import jax
import jax.numpy as jnp
from jax import lax

D = 16384
HQ = 128
KVH = 8
HD = 128
FF = 26624
PAGE = 64
ROWS = 4
SEQ = 2048
GQ = 16
BATCH = 16
SPAN = 1024
PPS = 16
POOL = 64
N_REPLICA = 4
N_FFN = 2


def draw_k_cache(key, part):
    full_shape = (N_REPLICA * N_FFN * POOL, PAGE, KVH * HD)
    drawn = jnp.clip(jax.random.normal(jax.random.fold_in(key, 1), full_shape, jnp.float32), -6.0, 6.0)
    return drawn.astype(jnp.bfloat16)


def draw_queries(key, part):
    full_shape = (BATCH, HQ * HD)
    drawn = jnp.clip(2.0 * jax.random.normal(jax.random.fold_in(key, 2), full_shape, jnp.float32), -12.0, 12.0)
    return drawn.astype(jnp.bfloat16)


def draw_page_table(key, part):
    subkeys = jax.random.split(key, N_REPLICA * N_FFN)
    orders = jax.vmap(lambda subkey: jax.random.permutation(subkey, POOL))(subkeys)
    orders = orders.reshape(N_REPLICA, N_FFN, ROWS, PPS).transpose(0, 2, 1, 3).reshape(BATCH, N_FFN * PPS)
    return orders.astype(jnp.int32)


def draw_seq_lens(key, part):
    lengths = jax.random.randint(key, (BATCH,), 1, SEQ + 1, dtype=jnp.int32)
    return lengths.at[0].set(SEQ).astype(jnp.int32)


def draw_residual(key, part):
    first_key, second_key, third_key = jax.random.split(key, 3)
    row_scale = jnp.exp(jax.random.uniform(first_key, (BATCH, 1), jnp.float32, math.log(0.3), math.log(3.0)))
    column_pos = jnp.arange(D, dtype=jnp.float32).reshape(1, D) / D
    column_scale = 0.1 * jnp.power(10.0, column_pos) * jax.random.uniform(second_key, (1, D), jnp.float32, 0.7, 1.4)
    drawn = jnp.clip(jax.random.normal(third_key, (BATCH, D), jnp.float32), -4.0, 4.0)
    return (drawn * row_scale * column_scale).astype(jnp.bfloat16)


def levels(rng, extent, cuts, smallest, largest):
    factor_of, own = 1.0, jax.random.fold_in(rng, 6)
    for axis_at, shards_of in cuts:
        heights = jnp.exp(jax.random.uniform(jax.random.fold_in(own, axis_at), (shards_of,), jnp.float32, smallest / len(cuts), largest / len(cuts)))
        factor_of = factor_of * jnp.repeat(heights, extent[axis_at] // shards_of).reshape([-1 if axis == axis_at else 1 for axis in range(len(extent))])
    return factor_of


def scatter_about(stream_key, dims, scale, limit, cuts=(), held_as=jnp.bfloat16):
    values = scale * jax.random.normal(stream_key, dims, jnp.float32)
    if cuts:
        values = values * levels(stream_key, dims, cuts, -0.22, 0.18)
    return jnp.clip(values, -limit, limit).astype(held_as)


def setup_inputs(seed: int = 0) -> dict:
    streams_of = jax.random.split(jax.random.key(seed), 11)
    queries = draw_queries(jax.random.fold_in(streams_of[10], 71), 0)
    k_cache = draw_k_cache(jax.random.fold_in(streams_of[10], 71), 0)
    v_cache = scatter_about(streams_of[2], (N_REPLICA * N_FFN * POOL, PAGE, KVH * HD), 1.0, 6.0, ((0, 8), (2, 4)))
    page_table = draw_page_table(jax.random.fold_in(streams_of[10], 71), 0)
    seq_lens = draw_seq_lens(jax.random.fold_in(streams_of[10], 71), 0)
    out_proj = scatter_about(streams_of[5], (HQ * HD, D), (HQ * HD // 8) ** -0.5, 0.125, ((0, 4), (1, 8)))
    residual = draw_residual(jax.random.fold_in(streams_of[10], 71), 0)
    norm_gain = jnp.clip(1.0 + 0.18 * jax.random.normal(streams_of[7], (D,), jnp.float32), 0.099609375, 1.8984375).astype(jnp.bfloat16)
    gate_weight = scatter_about(streams_of[8], (FF, D), D ** -0.5, 0.046875, ((0, 32),))
    up_weight = scatter_about(streams_of[9], (FF, D), D ** -0.5, 0.046875, ((0, 32),))
    return dict(queries=queries, k_cache=k_cache, v_cache=v_cache, page_table=page_table, seq_lens=seq_lens, out_proj=out_proj, residual=residual, norm_gain=norm_gain, gate_weight=gate_weight, up_weight=up_weight)


NEG_FILL = -1e+30
NORM_EPS = 1e-05

def reference(queries, k_cache, v_cache, page_table, seq_lens, out_proj, residual, norm_gain, gate_weight, up_weight):
    score_scale = 1.0 / math.sqrt(HD)
    column_ids = jnp.arange(N_FFN * PPS, dtype=jnp.int32)
    positions = jnp.arange(SEQ, dtype=jnp.int32)

    def attend_row(row_index):
        replica_id = row_index // ROWS
        page_ids = ((replica_id * N_FFN + column_ids // PPS) * POOL + page_table[row_index]).astype(jnp.int32)
        key_rows = k_cache[page_ids].astype(jnp.float32).reshape(N_FFN, SPAN, KVH, HD)
        value_rows = v_cache[page_ids].astype(jnp.float32).reshape(N_FFN, SPAN, KVH, HD)
        query_heads = queries[row_index].astype(jnp.float32).reshape(KVH, GQ, HD)
        scores = jnp.einsum('kgd,fskd->kgfs', query_heads, key_rows, precision=lax.Precision.HIGHEST) * score_scale
        visible = (positions < seq_lens[row_index]).reshape(1, 1, N_FFN, SPAN)
        block_max = lax.optimization_barrier(jnp.max(jnp.where(visible, scores, NEG_FILL), axis=-1))
        weights = jnp.where(visible, jnp.exp(scores - block_max[..., None]), 0.0)
        block_total = lax.optimization_barrier(jnp.sum(weights, axis=-1))
        rounded = lax.optimization_barrier(weights.astype(jnp.bfloat16)).astype(jnp.float32)
        block_out = jnp.einsum('kgfs,fskd->kgfd', rounded, value_rows, precision=lax.Precision.HIGHEST)
        overall = lax.optimization_barrier(jnp.max(block_max, axis=-1))
        factor = jnp.exp(block_max - overall[..., None])
        denominator = lax.optimization_barrier(jnp.sum(block_total * factor, axis=-1))
        weighted = lax.optimization_barrier(jnp.sum(block_out * factor[..., None], axis=2))
        return (weighted / denominator[..., None]).astype(jnp.bfloat16).reshape(HQ * HD)
    contexts = lax.map(attend_row, jnp.arange(BATCH, dtype=jnp.int32))
    attention = jnp.dot(contexts, out_proj, preferred_element_type=jnp.float32)
    post_attn = (residual.astype(jnp.float32) + attention).astype(jnp.bfloat16)
    widened = post_attn.astype(jnp.float32)
    inverse = lax.rsqrt(lax.optimization_barrier(jnp.mean(widened * widened, axis=1)) + NORM_EPS)
    normed = (widened * inverse[:, None] * norm_gain.astype(jnp.float32)).astype(jnp.bfloat16)
    gate_part = jnp.dot(normed, gate_weight.T, preferred_element_type=jnp.float32)
    up_part = jnp.dot(normed, up_weight.T, preferred_element_type=jnp.float32)
    hidden = (jax.nn.silu(gate_part) * up_part).astype(jnp.bfloat16)
    return (post_attn, hidden)
```

```python
import functools
import math

import jax
import jax.numpy as jnp
from jax import lax
from jax.experimental import pallas as pl
from jax.experimental.pallas import tpu as pltpu
from jax.sharding import PartitionSpec as P

D = 16384
HD = 128
GQ = 16


NEG_FILL = -1e30
NORM_EPS = 1e-05
MESH = pl.DeviceIdType.MESH
VMEM_BYTES = 67043328
F32 = jnp.float32
BF16 = jnp.bfloat16
NT = (((1,), (1,)), ((), ()))


def merged(part, axis, combine):
    gathered = jax.tree.map(lambda a: lax.all_gather(a, axis), part)

    def take(source):
        return jax.tree.map(lambda a: lax.dynamic_index_in_dim(a, source, 0, False), gathered)

    return lax.fori_loop(
        1, lax.axis_size(axis), lambda source, state: combine(state, take(source)), take(0)
    )


def join_parts(earlier, later):
    first_max, first_total, first_out = earlier
    second_max, second_total, second_out = later
    overall = jnp.maximum(first_max, second_max)
    first_factor = jnp.exp(first_max - overall)
    second_factor = jnp.exp(second_max - overall)
    joined_total = first_total * first_factor + second_total * second_factor
    joined_out = first_out * first_factor[..., None] + second_out * second_factor[..., None]
    return (overall, joined_total, joined_out)


def general_path(
    queries,
    k_cache,
    v_cache,
    page_table,
    seq_lens,
    out_proj,
    residual,
    norm_gain,
    gate_weight,
    up_weight,
):
    score_scale = 1.0 / math.sqrt(HD)
    row_count = queries.shape[0]
    local_heads = k_cache.shape[2] // HD
    span_len = page_table.shape[1] * k_cache.shape[1]
    key_rows = k_cache[page_table].reshape(row_count, span_len, local_heads, HD)
    value_rows = v_cache[page_table].reshape(row_count, span_len, local_heads, HD)
    query_heads = queries.reshape(row_count, local_heads, GQ, HD)
    scores = (
        jnp.einsum("rkgd,rskd->rkgs", query_heads, key_rows, preferred_element_type=jnp.float32)
        * score_scale
    )
    positions = lax.axis_index("ffn") * span_len + jnp.arange(span_len, dtype=jnp.int32)
    visible = (positions[None, :] < seq_lens[:, None])[:, None, None, :]
    block_max = jnp.max(jnp.where(visible, scores, NEG_FILL), axis=-1)
    weights = jnp.where(visible, jnp.exp(scores - block_max[..., None]), 0.0)
    block_total = jnp.sum(weights, axis=-1)
    block_out = jnp.einsum(
        "rkgs,rskd->rkgd",
        weights.astype(jnp.bfloat16),
        value_rows,
        preferred_element_type=jnp.float32,
    )
    overall, denominator, weighted = merged((block_max, block_total, block_out), "ffn", join_parts)
    contexts = (
        (weighted / denominator[..., None])
        .astype(jnp.bfloat16)
        .reshape(row_count, local_heads * GQ * HD)
    )
    partial_value = jnp.dot(
        lax.all_gather(contexts, "replica", axis=0, tiled=True),
        out_proj,
        preferred_element_type=jnp.float32,
    )
    own_count = residual.shape[0]
    own_first = lax.axis_index("kvhead") * own_count
    own_part = lax.dynamic_slice_in_dim(partial_value, own_first, own_count, 0) + residual.astype(
        jnp.float32
    )
    partial_value = lax.dynamic_update_slice_in_dim(partial_value, own_part, own_first, 0)
    gain_wide = norm_gain.astype(jnp.float32)
    summed = lax.psum(partial_value, "kvhead")
    post_all = summed.astype(jnp.bfloat16)
    post_attn = lax.dynamic_slice_in_dim(post_all, own_first, own_count, 0)
    widened = post_all.astype(jnp.float32)
    squares = lax.psum(jnp.sum(widened * widened, axis=1), ("replica", "ffn"))
    normed = (widened * lax.rsqrt(squares / D + NORM_EPS)[:, None] * gain_wide).astype(jnp.bfloat16)
    contract = (((1,), (1,)), ((), ()))
    shard_cols = lax.all_gather(normed, ("replica", "ffn"), axis=1, tiled=True)
    gate_sum = lax.dot_general(
        shard_cols, gate_weight, contract, preferred_element_type=jnp.float32
    )
    up_sum = lax.dot_general(shard_cols, up_weight, contract, preferred_element_type=jnp.float32)
    hidden = (jax.nn.silu(gate_sum) * up_sum).astype(jnp.bfloat16)
    return (post_attn, hidden)


def layer_kernel(
    sizes,
    page_ref,
    len_ref,
    query_ref,
    resid_ref,
    gain_ref,
    k_hbm,
    v_hbm,
    proj_hbm,
    gate_hbm,
    up_hbm,
    post_ref,
    hidden_ref,
    k_buf,
    v_buf,
    slots,
    q_heads,
    o_heads,
    stat_cols,
    stats,
    ctx_parts,
    ctx_wide,
    part,
    z_parts,
    blocks,
    gains,
    x_buf,
    gate_acc,
    up_acc,
    kv_sem,
    slot_sem,
    stat_send,
    stat_recv,
    ctx_send,
    ctx_recv,
    gain_send,
    gain_recv,
    z_send,
    z_recv,
    blk_send,
    blk_recv,
    fwd_send,
):
    n_rep, n_kv, n_ffn, n_slots, proj_rows = sizes
    replica = lax.axis_index("replica")
    kvhead = lax.axis_index("kvhead")
    ffn = lax.axis_index("ffn")
    rows, width = query_ref.shape
    heads = width // HD
    page_len = k_hbm.shape[1]
    kv_heads = k_hbm.shape[2] // HD
    pages = page_ref.shape[1]
    span = pages * page_len
    depth, cols = proj_hbm.shape
    all_rows = n_rep * rows
    own_rows = resid_ref.shape[0]
    n_chip = n_rep // 2
    chip, core = replica // 2, replica % 2

    def shard_of(rep, f):
        return rep * n_ffn + f

    me = shard_of(replica, ffn)

    def send(ref, index, sem_out, sem_in, target):
        return pltpu.make_async_remote_copy(
            src_ref=ref.at[index],
            dst_ref=ref.at[index],
            send_sem=sem_out,
            recv_sem=sem_in,
            device_id=target,
            device_id_type=MESH,
        )

    plane = []
    for a in range(n_chip):
        for c in range(2):
            for b in range(n_ffn):
                if (a, c, b) != (0, 0, 0):
                    rep = ((chip + a) % n_chip) * 2 + (core + c) % 2
                    plane.append((rep, (ffn + b) % n_ffn))
    lines = [(kvhead + k) % n_kv for k in range(1, n_kv)]

    k_copy = pltpu.make_async_copy(k_hbm, k_buf, kv_sem.at[0])
    v_copy = pltpu.make_async_copy(v_hbm, v_buf, kv_sem.at[1])
    k_copy.start()
    v_copy.start()
    proj_copies = []
    for i, first in enumerate(range(0, depth, proj_rows)):
        count = min(proj_rows, depth - first)
        copy = pltpu.make_async_copy(
            proj_hbm.at[pl.ds(first, count), :], slots.at[i, pl.ds(0, count), :], slot_sem.at[i]
        )
        copy.start()
        proj_copies.append((copy, first, count))
    n_proj = len(proj_copies)

    direct = []
    for a in range(n_chip):
        for b in range(n_ffn):
            direct.append((a, b))
    direct.sort(key=lambda ab: (ab[0] + ab[1], ab[0]))
    order = [(0, 0, 0), (0, 0, 1)]
    order += [(a, b, 0) for a, b in direct[1:]] + [(a, b, 1) for a, b in direct[1:]]

    def place(a, b, c):
        rep = ((chip + a) % n_chip) * 2 + (core + c) % 2
        return rep, (ffn + b) % n_ffn

    weight_copies = []
    for step, where in enumerate(order):
        shard = shard_of(*place(*where))
        window = pl.ds(pl.multiple_of(shard * cols, cols), cols)
        for which, source in enumerate((gate_hbm, up_hbm)):
            slot = (n_proj + 2 * step + which) % n_slots
            weight_copies.append(
                pltpu.make_async_copy(source.at[:, window], slots.at[slot, pl.ds(0, source.shape[0]), :], slot_sem.at[slot])
            )
    early = n_slots - n_proj
    for copy in weight_copies[:early]:
        copy.start()

    barrier = pltpu.get_barrier_semaphore()
    for rep, f in plane:
        pl.semaphore_signal(
            barrier, inc=1, device_id={"replica": rep, "ffn": f}, device_id_type=MESH
        )
    for k in lines:
        pl.semaphore_signal(barrier, inc=1, device_id={"kvhead": k}, device_id_type=MESH)

    for h in range(heads):
        q_heads[pl.ds(h, rows, stride=heads), :] = query_ref[:, h * HD : (h + 1) * HD].astype(F32)
    gains[me] = gain_ref[...].astype(F32)

    pl.semaphore_wait(barrier, len(plane) + len(lines))

    gain_copies = []
    for i, (rep, f) in enumerate(plane):
        copy = send(gains, me, gain_send.at[i], gain_recv.at[me], {"replica": rep, "ffn": f})
        copy.start()
        gain_copies.append(copy)

    scale = 1.0 / math.sqrt(HD)
    position = ffn * span + lax.broadcasted_iota(jnp.int32, (GQ, span), 1)
    lane = lax.broadcasted_iota(jnp.int32, (GQ, HD), 1)
    k_copy.wait()
    weights = []
    for r in range(rows):
        visible = position < len_ref[r]
        for g in range(kv_heads):
            keys = jnp.concatenate(
                [k_buf[page_ref[r, j], :, g * HD : (g + 1) * HD] for j in range(pages)], axis=0
            )
            first = (r * kv_heads + g) * GQ
            query = q_heads[first : first + GQ, :].astype(BF16)
            scores = lax.dot_general(query, keys, NT, preferred_element_type=F32) * scale
            top = jnp.max(jnp.where(visible, scores, NEG_FILL), axis=1, keepdims=True)
            weight = jnp.where(visible, jnp.exp(scores - top), 0.0)
            total = jnp.sum(weight, axis=1, keepdims=True)
            stat_cols[first : first + GQ, :] = jnp.where(
                lane < HD // 2,
                jnp.broadcast_to(top, (GQ, HD)),
                jnp.broadcast_to(total, (GQ, HD)),
            )
            weights.append(weight.astype(BF16))
    turned = stat_cols[...].T
    stats[0, 0:1, :] = turned[0:1, :]
    stats[0, 1:2, :] = turned[HD // 2 : HD // 2 + 1, :]
    stat_copy = pltpu.make_async_remote_copy(
        src_ref=stats.at[0],
        dst_ref=stats.at[1],
        send_sem=stat_send,
        recv_sem=stat_recv,
        device_id={"ffn": (ffn + 1) % n_ffn},
        device_id_type=MESH,
    )
    stat_copy.start()
    v_copy.wait()
    for r in range(rows):
        for g in range(kv_heads):
            values = jnp.concatenate(
                [v_buf[page_ref[r, j], :, g * HD : (g + 1) * HD] for j in range(pages)], axis=0
            )
            first = (r * kv_heads + g) * GQ
            o_heads[first : first + GQ, :] = jnp.dot(
                weights[r * kv_heads + g], values, preferred_element_type=F32
            )
    stat_copy.wait()
    own_top, own_total = stats[0, 0:1, :], stats[0, 1:2, :]
    far_top, far_total = stats[1, 0:1, :], stats[1, 1:2, :]
    overall = jnp.maximum(own_top, far_top)
    own_lift = jnp.exp(own_top - overall)
    far_lift = jnp.exp(far_top - overall)
    factor = own_lift / (own_lift * own_total + far_lift * far_total)
    o_heads[...] = o_heads[...] * jnp.broadcast_to(factor, (HD, HD)).T
    for h in range(heads):
        ctx_parts[me, :, h * HD : (h + 1) * HD] = o_heads[
            pl.ds(h, rows, stride=heads), :
        ].astype(BF16)
    ctx_copies = []
    for i, (rep, f) in enumerate(plane):
        copy = send(ctx_parts, me, ctx_send.at[i], ctx_recv.at[me], {"replica": rep, "ffn": f})
        copy.start()
        ctx_copies.append(copy)
    for rep, f in plane:
        shard = shard_of(rep, f)
        send(
            ctx_parts, shard, ctx_send.at[0], ctx_recv.at[shard], {"replica": rep, "ffn": f}
        ).wait_recv()
    for rep in range(n_rep):
        joined = ctx_parts[rep * n_ffn].astype(F32)
        for f in range(1, n_ffn):
            joined = joined + ctx_parts[rep * n_ffn + f].astype(F32)
        ctx_wide[rep * rows : (rep + 1) * rows, :] = joined

    total = None
    for i, (copy, first, count) in enumerate(proj_copies):
        copy.wait()
        term = jnp.dot(
            ctx_wide[:, first : first + count].astype(BF16),
            slots[i, 0:count, :],
            preferred_element_type=F32,
        )
        if i == 0:
            part[...] = term
        else:
            part[...] += term
    for copy in weight_copies[early:]:
        copy.start()
    resid = resid_ref[...].astype(F32)
    for k in range(n_kv):
        part[k * own_rows : (k + 1) * own_rows, :] += jnp.where(kvhead == k, resid, 0.0)
    z_parts[kvhead] = part[...].astype(BF16)
    z_copies = []
    for i, k in enumerate(lines):
        copy = send(z_parts, kvhead, z_send.at[i], z_recv.at[kvhead], {"kvhead": k})
        copy.start()
        z_copies.append(copy)
    gate_acc[...] = jnp.zeros_like(gate_acc)
    up_acc[...] = jnp.zeros_like(up_acc)
    for copy in gain_copies:
        copy.wait_send()
    for rep, f in plane:
        shard = shard_of(rep, f)
        send(
            gains, shard, gain_send.at[0], gain_recv.at[shard], {"replica": rep, "ffn": f}
        ).wait_recv()
    for copy in ctx_copies:
        copy.wait_send()
    for k in lines:
        send(z_parts, k, z_send.at[0], z_recv.at[k], {"kvhead": k}).wait_recv()
        part[...] += z_parts[k].astype(F32)
    blocks[me] = part[...].astype(BF16)
    blk_copies = []
    for i, where in enumerate([(0, 0, 1)] + [(a, b, 0) for a, b in direct[1:]]):
        rep, f = place(*where)
        copy = send(blocks, me, blk_send.at[i], blk_recv.at[me], {"replica": rep, "ffn": f})
        copy.start()
        blk_copies.append(copy)
    own_post = jnp.zeros((own_rows, cols), F32)
    for k in range(n_kv):
        own_post = own_post + jnp.where(
            kvhead == k, part[k * own_rows : (k + 1) * own_rows, :], 0.0
        )
    post_ref[...] = own_post.astype(BF16)

    def arrive(where):
        rep, f = place(*where)
        shard = shard_of(rep, f)
        send(
            blocks, shard, blk_send.at[0], blk_recv.at[shard], {"replica": rep, "ffn": f}
        ).wait_recv()

    fwd_copies = []

    def pass_on(where):
        arrive(where)
        shard = shard_of(*place(*where))
        copy = send(
            blocks,
            shard,
            fwd_send.at[len(fwd_copies)],
            blk_recv.at[shard],
            {"replica": chip * 2 + (core + 1) % 2},
        )
        copy.start()
        fwd_copies.append(copy)

    squares = jnp.zeros((all_rows, 1), F32)
    pending = [(a, b, 0) for a, b in direct[1:]]
    piece = 512 if cols % 512 == 0 else cols
    for step, where in enumerate(order):
        if step >= 1 and pending:
            pass_on(pending.pop(0))
            if pending:
                pass_on(pending.pop(0))
        if where[2] == 1:
            arrive(where)
        shard = shard_of(*place(*where))
        wide = blocks[shard].astype(F32)
        squares = squares + jnp.sum(wide * wide, axis=1, keepdims=True)
        x_buf[...] = (wide * gains[shard]).astype(BF16)
        weight_copies[2 * step].wait()
        weight_copies[2 * step + 1].wait()
        gate_slot = (n_proj + 2 * step) % n_slots
        up_slot = (n_proj + 2 * step + 1) % n_slots

        def accumulate(i, carry, gate_slot=gate_slot, up_slot=up_slot):
            window = pl.ds(pl.multiple_of(i * piece, piece), piece)
            part_x = x_buf[:, window]
            units = gate_acc.shape[1]
            gate_acc[...] += lax.dot_general(
                part_x, slots[gate_slot, 0:units, window], NT, preferred_element_type=F32
            )
            up_acc[...] += lax.dot_general(
                part_x, slots[up_slot, 0:units, window], NT, preferred_element_type=F32
            )
            return carry

        lax.fori_loop(0, cols // piece, accumulate, 0)
    inverse = lax.rsqrt(squares / D + NORM_EPS)
    gate = gate_acc[...] * inverse
    hidden_ref[...] = (gate / (1.0 + jnp.exp(-gate)) * (up_acc[...] * inverse)).astype(BF16)
    for copy in z_copies + blk_copies + fwd_copies:
        copy.wait_send()


def plan(n_rep, n_kv, n_ffn, shapes):
    queries, k_cache, v_cache, page_table, seq_lens, out_proj, residual, gain, gate, up = shapes
    depth, cols = out_proj
    units = gate[0]
    rows = queries[0]
    heads = queries[1] // HD
    if n_ffn != 2 or n_rep % 2 or units % 16 or cols % 256 or rows * heads != HD:
        return None
    if gate[1] != n_rep * n_ffn * cols or page_table[0] * page_table[1] != k_cache[0]:
        return None
    proj_rows = units // 256 * 256
    if proj_rows == 0:
        return None
    n_slots = 2 * n_rep * n_ffn
    n_proj = -(-depth // proj_rows)
    held = n_slots * units * cols * 2 + 4 * math.prod(k_cache)
    if n_proj > n_slots or held + (4 << 20) > VMEM_BYTES:
        return None
    return n_slots, proj_rows


def per_device(sizes, *args):
    (queries, k_cache, v_cache, page_table, seq_lens, out_proj, residual, gain, gate, up) = args
    n_rep, n_kv, n_ffn = sizes
    found = plan(n_rep, n_kv, n_ffn, [a.shape for a in args])
    if found is None:
        return general_path(*args)
    n_slots, proj_rows = found
    rows, width = queries.shape
    cols = out_proj.shape[1]
    units = gate.shape[0]
    all_rows = n_rep * rows
    shards = n_rep * n_ffn
    chips = shards // 2
    vmem = pl.BlockSpec(memory_space=pltpu.VMEM)
    smem = pl.BlockSpec(memory_space=pltpu.SMEM)
    hbm = pl.BlockSpec(memory_space=pl.ANY)
    dma = pltpu.SemaphoreType.DMA
    return pl.pallas_call(
        functools.partial(layer_kernel, (n_rep, n_kv, n_ffn, n_slots, proj_rows)),
        out_shape=(
            jax.ShapeDtypeStruct(residual.shape, BF16),
            jax.ShapeDtypeStruct((all_rows, units), BF16),
        ),
        in_specs=[smem, smem, vmem, vmem, vmem] + [hbm] * 5,
        out_specs=(vmem, vmem),
        scratch_shapes=[
            pltpu.VMEM(k_cache.shape, BF16),
            pltpu.VMEM(v_cache.shape, BF16),
            pltpu.VMEM((n_slots, units, cols), BF16),
            pltpu.VMEM((HD, HD), F32),
            pltpu.VMEM((HD, HD), F32),
            pltpu.VMEM((HD, HD), F32),
            pltpu.VMEM((2, 8, HD), F32),
            pltpu.VMEM((shards, rows, width), BF16),
            pltpu.VMEM((all_rows, width), F32),
            pltpu.VMEM((all_rows, cols), F32),
            pltpu.VMEM((n_kv, all_rows, cols), BF16),
            pltpu.VMEM((shards, all_rows, cols), BF16),
            pltpu.VMEM((shards, 1, cols), F32),
            pltpu.VMEM((all_rows, cols), BF16),
            pltpu.VMEM((all_rows, units), F32),
            pltpu.VMEM((all_rows, units), F32),
            dma((2,)),
            dma((n_slots,)),
            dma,
            dma,
            dma((shards - 1,)),
            dma((shards,)),
            dma((shards - 1,)),
            dma((shards,)),
            dma((n_kv - 1,)),
            dma((n_kv,)),
            dma((chips,)),
            dma((shards,)),
            dma((max(chips - 1, 1),)),
        ],
        compiler_params=pltpu.CompilerParams(
            collective_id=0, has_side_effects=True, vmem_limit_bytes=VMEM_BYTES - (1 << 20)
        ),
    )(
        page_table,
        seq_lens,
        queries,
        residual,
        gain.reshape(1, cols),
        k_cache,
        v_cache,
        out_proj,
        gate,
        up,
    )


def solution(mesh):
    in_specs = (
        P("replica", "kvhead"),
        P(("replica", "ffn"), None, "kvhead"),
        P(("replica", "ffn"), None, "kvhead"),
        P("replica", "ffn"),
        P("replica"),
        P("kvhead", ("replica", "ffn")),
        P("kvhead", ("replica", "ffn")),
        P(("replica", "ffn")),
        P(("replica", "kvhead", "ffn"), None),
        P(("replica", "kvhead", "ffn"), None),
    )
    out_specs = (P("kvhead", ("replica", "ffn")), P(None, ("replica", "kvhead", "ffn")))
    sizes = (mesh.shape["replica"], mesh.shape["kvhead"], mesh.shape["ffn"])
    return jax.shard_map(
        functools.partial(per_device, sizes),
        mesh=mesh,
        in_specs=in_specs,
        out_specs=out_specs,
        check_vma=False,
    )
```

```python
import functools
import math

import jax
import jax.numpy as jnp
from jax import lax
from jax.experimental import pallas as pl
from jax.experimental.pallas import tpu as pltpu
from jax.sharding import PartitionSpec as P

D = 16384
HD = 128
GQ = 16


NEG_FILL = -1e30
NORM_EPS = 1e-05
MESH = pl.DeviceIdType.MESH
VMEM_BYTES = 67043328
F32 = jnp.float32
BF16 = jnp.bfloat16
NT = (((1,), (1,)), ((), ()))


def merged(part, axis, combine):
    gathered = jax.tree.map(lambda a: lax.all_gather(a, axis), part)

    def take(source):
        return jax.tree.map(lambda a: lax.dynamic_index_in_dim(a, source, 0, False), gathered)

    return lax.fori_loop(
        1, lax.axis_size(axis), lambda source, state: combine(state, take(source)), take(0)
    )


def join_parts(earlier, later):
    first_max, first_total, first_out = earlier
    second_max, second_total, second_out = later
    overall = jnp.maximum(first_max, second_max)
    first_factor = jnp.exp(first_max - overall)
    second_factor = jnp.exp(second_max - overall)
    joined_total = first_total * first_factor + second_total * second_factor
    joined_out = first_out * first_factor[..., None] + second_out * second_factor[..., None]
    return (overall, joined_total, joined_out)


def general_path(
    queries,
    k_cache,
    v_cache,
    page_table,
    seq_lens,
    out_proj,
    residual,
    norm_gain,
    gate_weight,
    up_weight,
):
    score_scale = 1.0 / math.sqrt(HD)
    row_count = queries.shape[0]
    local_heads = k_cache.shape[2] // HD
    span_len = page_table.shape[1] * k_cache.shape[1]
    key_rows = k_cache[page_table].reshape(row_count, span_len, local_heads, HD)
    value_rows = v_cache[page_table].reshape(row_count, span_len, local_heads, HD)
    query_heads = queries.reshape(row_count, local_heads, GQ, HD)
    scores = (
        jnp.einsum("rkgd,rskd->rkgs", query_heads, key_rows, preferred_element_type=jnp.float32)
        * score_scale
    )
    positions = lax.axis_index("ffn") * span_len + jnp.arange(span_len, dtype=jnp.int32)
    visible = (positions[None, :] < seq_lens[:, None])[:, None, None, :]
    block_max = jnp.max(jnp.where(visible, scores, NEG_FILL), axis=-1)
    weights = jnp.where(visible, jnp.exp(scores - block_max[..., None]), 0.0)
    block_total = jnp.sum(weights, axis=-1)
    block_out = jnp.einsum(
        "rkgs,rskd->rkgd",
        weights.astype(jnp.bfloat16),
        value_rows,
        preferred_element_type=jnp.float32,
    )
    overall, denominator, weighted = merged((block_max, block_total, block_out), "ffn", join_parts)
    contexts = (
        (weighted / denominator[..., None])
        .astype(jnp.bfloat16)
        .reshape(row_count, local_heads * GQ * HD)
    )
    partial_value = jnp.dot(
        lax.all_gather(contexts, "replica", axis=0, tiled=True),
        out_proj,
        preferred_element_type=jnp.float32,
    )
    own_count = residual.shape[0]
    own_first = lax.axis_index("kvhead") * own_count
    own_part = lax.dynamic_slice_in_dim(partial_value, own_first, own_count, 0) + residual.astype(
        jnp.float32
    )
    partial_value = lax.dynamic_update_slice_in_dim(partial_value, own_part, own_first, 0)
    gain_wide = norm_gain.astype(jnp.float32)
    summed = lax.psum(partial_value, "kvhead")
    post_all = summed.astype(jnp.bfloat16)
    post_attn = lax.dynamic_slice_in_dim(post_all, own_first, own_count, 0)
    widened = post_all.astype(jnp.float32)
    squares = lax.psum(jnp.sum(widened * widened, axis=1), ("replica", "ffn"))
    normed = (widened * lax.rsqrt(squares / D + NORM_EPS)[:, None] * gain_wide).astype(jnp.bfloat16)
    contract = (((1,), (1,)), ((), ()))
    shard_cols = lax.all_gather(normed, ("replica", "ffn"), axis=1, tiled=True)
    gate_sum = lax.dot_general(
        shard_cols, gate_weight, contract, preferred_element_type=jnp.float32
    )
    up_sum = lax.dot_general(shard_cols, up_weight, contract, preferred_element_type=jnp.float32)
    hidden = (jax.nn.silu(gate_sum) * up_sum).astype(jnp.bfloat16)
    return (post_attn, hidden)


def layer_kernel(
    sizes,
    page_ref,
    len_ref,
    query_ref,
    resid_ref,
    gain_ref,
    k_hbm,
    v_hbm,
    proj_hbm,
    gate_hbm,
    up_hbm,
    post_ref,
    hidden_ref,
    k_buf,
    v_buf,
    slots,
    q_heads,
    o_heads,
    stat_cols,
    stats,
    ctx_parts,
    ctx_wide,
    part,
    z_parts,
    blocks,
    gains,
    x_buf,
    gate_acc,
    up_acc,
    kv_sem,
    slot_sem,
    stat_send,
    stat_recv,
    ctx_send,
    ctx_recv,
    gain_send,
    gain_recv,
    z_send,
    z_recv,
    blk_send,
    blk_recv,
    fwd_send,
):
    n_rep, n_kv, n_ffn, n_slots, proj_rows = sizes
    replica = lax.axis_index("replica")
    kvhead = lax.axis_index("kvhead")
    ffn = lax.axis_index("ffn")
    rows, width = query_ref.shape
    heads = width // HD
    page_len = k_hbm.shape[1]
    kv_heads = k_hbm.shape[2] // HD
    pages = page_ref.shape[1]
    span = pages * page_len
    depth, cols = proj_hbm.shape
    all_rows = n_rep * rows
    own_rows = resid_ref.shape[0]
    n_chip = n_rep // 2
    chip, core = replica // 2, replica % 2

    def shard_of(rep, f):
        return rep * n_ffn + f

    me = shard_of(replica, ffn)

    def send(ref, index, sem_out, sem_in, target):
        return pltpu.make_async_remote_copy(
            src_ref=ref.at[index],
            dst_ref=ref.at[index],
            send_sem=sem_out,
            recv_sem=sem_in,
            device_id=target,
            device_id_type=MESH,
        )

    plane = []
    for a in range(n_chip):
        for c in range(2):
            for b in range(n_ffn):
                if (a, c, b) != (0, 0, 0):
                    rep = ((chip + a) % n_chip) * 2 + (core + c) % 2
                    plane.append((rep, (ffn + b) % n_ffn))
    lines = [(kvhead + k) % n_kv for k in range(1, n_kv)]

    k_copy = pltpu.make_async_copy(k_hbm, k_buf, kv_sem.at[0])
    v_copy = pltpu.make_async_copy(v_hbm, v_buf, kv_sem.at[1])
    k_copy.start()
    v_copy.start()
    proj_copies = []
    for i, first in enumerate(range(0, depth, proj_rows)):
        count = min(proj_rows, depth - first)
        copy = pltpu.make_async_copy(
            proj_hbm.at[pl.ds(first, count), :], slots.at[i, pl.ds(0, count), :], slot_sem.at[i]
        )
        proj_copies.append((copy, first, count))
    n_proj = len(proj_copies)

    direct = []
    for a in range(n_chip):
        for b in range(n_ffn):
            direct.append((a, b))
    direct.sort(key=lambda ab: (ab[0] + ab[1], ab[0]))
    order = [(0, 0, 0), (0, 0, 1)]
    order += [(a, b, 0) for a, b in direct[1:]] + [(a, b, 1) for a, b in direct[1:]]

    def place(a, b, c):
        rep = ((chip + a) % n_chip) * 2 + (core + c) % 2
        return rep, (ffn + b) % n_ffn

    weight_copies = []
    for step, where in enumerate(order):
        shard = shard_of(*place(*where))
        window = pl.ds(pl.multiple_of(shard * cols, cols), cols)
        for which, source in enumerate((gate_hbm, up_hbm)):
            slot = (n_proj + 2 * step + which) % n_slots
            weight_copies.append(
                pltpu.make_async_copy(source.at[:, window], slots.at[slot, pl.ds(0, source.shape[0]), :], slot_sem.at[slot])
            )
    early = n_slots - n_proj
    opening = min(4, early)

    barrier = pltpu.get_barrier_semaphore()
    for rep, f in plane:
        pl.semaphore_signal(
            barrier, inc=1, device_id={"replica": rep, "ffn": f}, device_id_type=MESH
        )
    for k in lines:
        pl.semaphore_signal(barrier, inc=1, device_id={"kvhead": k}, device_id_type=MESH)

    for h in range(heads):
        q_heads[pl.ds(h, rows, stride=heads), :] = query_ref[:, h * HD : (h + 1) * HD].astype(F32)
    gains[me] = gain_ref[...].astype(F32).reshape(1, cols)

    pl.semaphore_wait(barrier, len(plane) + len(lines))

    gain_copies = []
    for i, (rep, f) in enumerate(plane):
        copy = send(gains, me, gain_send.at[i], gain_recv.at[me], {"replica": rep, "ffn": f})
        copy.start()
        gain_copies.append(copy)

    scale = 1.0 / math.sqrt(HD)
    position = ffn * span + lax.broadcasted_iota(jnp.int32, (GQ, span), 1)
    lane = lax.broadcasted_iota(jnp.int32, (GQ, HD), 1)
    k_copy.wait()
    for copy, _, _ in proj_copies:
        copy.start()
    weights = []
    for r in range(rows):
        visible = position < len_ref[r]
        for g in range(kv_heads):
            keys = jnp.concatenate(
                [k_buf[page_ref[r, j], :, g * HD : (g + 1) * HD] for j in range(pages)], axis=0
            )
            first = (r * kv_heads + g) * GQ
            query = q_heads[first : first + GQ, :].astype(BF16)
            scores = lax.dot_general(query, keys, NT, preferred_element_type=F32) * scale
            top = jnp.max(jnp.where(visible, scores, NEG_FILL), axis=1, keepdims=True)
            weight = jnp.where(visible, jnp.exp(scores - top), 0.0)
            total = jnp.sum(weight, axis=1, keepdims=True)
            stat_cols[first : first + GQ, :] = jnp.where(
                lane < HD // 2,
                jnp.broadcast_to(top, (GQ, HD)),
                jnp.broadcast_to(total, (GQ, HD)),
            )
            weights.append(weight.astype(BF16))
    turned = stat_cols[...].T
    stats[0, 0:1, :] = turned[0:1, :]
    stats[0, 1:2, :] = turned[HD // 2 : HD // 2 + 1, :]
    stat_copy = pltpu.make_async_remote_copy(
        src_ref=stats.at[0],
        dst_ref=stats.at[1],
        send_sem=stat_send,
        recv_sem=stat_recv,
        device_id={"ffn": (ffn + 1) % n_ffn},
        device_id_type=MESH,
    )
    stat_copy.start()
    v_copy.wait()
    for r in range(rows):
        for g in range(kv_heads):
            values = jnp.concatenate(
                [v_buf[page_ref[r, j], :, g * HD : (g + 1) * HD] for j in range(pages)], axis=0
            )
            first = (r * kv_heads + g) * GQ
            o_heads[first : first + GQ, :] = jnp.dot(
                weights[r * kv_heads + g], values, preferred_element_type=F32
            )
    stat_copy.wait()
    own_top, own_total = stats[0, 0:1, :], stats[0, 1:2, :]
    far_top, far_total = stats[1, 0:1, :], stats[1, 1:2, :]
    overall = jnp.maximum(own_top, far_top)
    own_lift = jnp.exp(own_top - overall)
    far_lift = jnp.exp(far_top - overall)
    factor = own_lift / (own_lift * own_total + far_lift * far_total)
    o_heads[...] = o_heads[...] * jnp.broadcast_to(factor, (HD, HD)).T
    for h in range(heads):
        ctx_parts[me, :, h * HD : (h + 1) * HD] = o_heads[
            pl.ds(h, rows, stride=heads), :
        ].astype(BF16)
    ctx_copies = []
    for i, (rep, f) in enumerate(plane):
        copy = send(ctx_parts, me, ctx_send.at[i], ctx_recv.at[me], {"replica": rep, "ffn": f})
        copy.start()
        ctx_copies.append(copy)
    for copy in weight_copies[:opening]:
        copy.start()
    for rep, f in plane:
        shard = shard_of(rep, f)
        send(
            ctx_parts, shard, ctx_send.at[0], ctx_recv.at[shard], {"replica": rep, "ffn": f}
        ).wait_recv()
    for rep in range(n_rep):
        joined = ctx_parts[rep * n_ffn].astype(F32)
        for f in range(1, n_ffn):
            joined = joined + ctx_parts[rep * n_ffn + f].astype(F32)
        ctx_wide[rep * rows : (rep + 1) * rows, :] = joined

    resid = resid_ref[...].astype(F32)
    half = cols // 2
    z_copies = []
    for side in range(2):
        window = slice(side * half, (side + 1) * half)
        for i, (copy, first, count) in enumerate(proj_copies):
            if side == 0:
                copy.wait()
            term = jnp.dot(
                ctx_wide[:, first : first + count].astype(BF16),
                slots[i, 0:count, window],
                preferred_element_type=F32,
            )
            if i == 0:
                part[:, window] = term
            else:
                part[:, window] += term
        if side == 0:
            for copy in weight_copies[opening:early]:
                copy.start()
        else:
            for copy in weight_copies[early:]:
                copy.start()
        for k in range(n_kv):
            part[k * own_rows : (k + 1) * own_rows, window] += jnp.where(
                kvhead == k, resid[:, window], 0.0
            )
        z_parts[kvhead, side] = part[:, window].astype(BF16)
        for i, k in enumerate(lines):
            copy = send(
                z_parts,
                (kvhead, side),
                z_send.at[side, i],
                z_recv.at[side, kvhead],
                {"kvhead": k},
            )
            copy.start()
            z_copies.append(copy)
    gate_acc[...] = jnp.zeros_like(gate_acc)
    up_acc[...] = jnp.zeros_like(up_acc)
    for copy in gain_copies:
        copy.wait_send()
    for rep, f in plane:
        shard = shard_of(rep, f)
        send(
            gains, shard, gain_send.at[0], gain_recv.at[shard], {"replica": rep, "ffn": f}
        ).wait_recv()
    for copy in ctx_copies:
        copy.wait_send()
    for side in range(2):
        for k in lines:
            send(
                z_parts, (k, side), z_send.at[side, 0], z_recv.at[side, k], {"kvhead": k}
            ).wait_recv()
            part[:, side * half : (side + 1) * half] += z_parts[k, side].astype(F32)
    blocks[me] = part[...].astype(BF16)
    blk_copies = []
    for i, where in enumerate([(0, 0, 1)] + [(a, b, 0) for a, b in direct[1:]]):
        rep, f = place(*where)
        copy = send(blocks, me, blk_send.at[i], blk_recv.at[me], {"replica": rep, "ffn": f})
        copy.start()
        blk_copies.append(copy)
    own_post = jnp.zeros((own_rows, cols), F32)
    for k in range(n_kv):
        own_post = own_post + jnp.where(
            kvhead == k, part[k * own_rows : (k + 1) * own_rows, :], 0.0
        )
    post_ref[...] = own_post.astype(BF16)

    def arrive(where):
        rep, f = place(*where)
        shard = shard_of(rep, f)
        send(
            blocks, shard, blk_send.at[0], blk_recv.at[shard], {"replica": rep, "ffn": f}
        ).wait_recv()

    fwd_copies = []

    def pass_on(where):
        arrive(where)
        shard = shard_of(*place(*where))
        copy = send(
            blocks,
            shard,
            fwd_send.at[len(fwd_copies)],
            blk_recv.at[shard],
            {"replica": chip * 2 + (core + 1) % 2},
        )
        copy.start()
        fwd_copies.append(copy)

    squares = jnp.zeros((all_rows, 1), F32)
    pending = [(a, b, 0) for a, b in direct[1:]]
    piece = 512 if cols % 512 == 0 else cols
    for step, where in enumerate(order):
        if step >= 1 and pending:
            pass_on(pending.pop(0))
            if pending:
                pass_on(pending.pop(0))
        if where[2] == 1:
            arrive(where)
        shard = shard_of(*place(*where))
        wide = blocks[shard].astype(F32)
        squares = squares + jnp.sum(wide * wide, axis=1, keepdims=True)
        x_buf[...] = (wide * gains[shard]).astype(BF16)
        weight_copies[2 * step].wait()
        weight_copies[2 * step + 1].wait()
        gate_slot = (n_proj + 2 * step) % n_slots
        up_slot = (n_proj + 2 * step + 1) % n_slots

        def accumulate(i, carry, gate_slot=gate_slot, up_slot=up_slot):
            window = pl.ds(pl.multiple_of(i * piece, piece), piece)
            part_x = x_buf[:, window]
            units = gate_acc.shape[1]
            gate_acc[...] += lax.dot_general(
                part_x, slots[gate_slot, 0:units, window], NT, preferred_element_type=F32
            )
            up_acc[...] += lax.dot_general(
                part_x, slots[up_slot, 0:units, window], NT, preferred_element_type=F32
            )
            return carry

        lax.fori_loop(0, cols // piece, accumulate, 0)
    inverse = lax.rsqrt(squares / D + NORM_EPS)
    gate = gate_acc[...] * inverse
    hidden_ref[...] = (gate / (1.0 + jnp.exp(-gate)) * (up_acc[...] * inverse)).astype(BF16)
    for copy in z_copies + blk_copies + fwd_copies:
        copy.wait_send()


def plan(n_rep, n_kv, n_ffn, shapes):
    queries, k_cache, v_cache, page_table, seq_lens, out_proj, residual, gain, gate, up = shapes
    depth, cols = out_proj
    units = gate[0]
    rows = queries[0]
    heads = queries[1] // HD
    if n_ffn != 2 or n_rep % 2 or units % 16 or cols % 256 or rows * heads != HD:
        return None
    if gate[1] != n_rep * n_ffn * cols or page_table[0] * page_table[1] != k_cache[0]:
        return None
    proj_rows = units // 256 * 256
    if proj_rows == 0:
        return None
    n_slots = 2 * n_rep * n_ffn
    n_proj = -(-depth // proj_rows)
    held = n_slots * units * cols * 2 + 4 * math.prod(k_cache)
    if n_proj > n_slots or held + (4 << 20) > VMEM_BYTES:
        return None
    return n_slots, proj_rows


def per_device(sizes, *args):
    (queries, k_cache, v_cache, page_table, seq_lens, out_proj, residual, gain, gate, up) = args
    n_rep, n_kv, n_ffn = sizes
    found = plan(n_rep, n_kv, n_ffn, [a.shape for a in args])
    if found is None:
        return general_path(*args)
    n_slots, proj_rows = found
    rows, width = queries.shape
    cols = out_proj.shape[1]
    units = gate.shape[0]
    all_rows = n_rep * rows
    shards = n_rep * n_ffn
    chips = shards // 2
    vmem = pl.BlockSpec(memory_space=pltpu.VMEM)
    smem = pl.BlockSpec(memory_space=pltpu.SMEM)
    hbm = pl.BlockSpec(memory_space=pl.ANY)
    dma = pltpu.SemaphoreType.DMA
    return pl.pallas_call(
        functools.partial(layer_kernel, (n_rep, n_kv, n_ffn, n_slots, proj_rows)),
        out_shape=(
            jax.ShapeDtypeStruct(residual.shape, BF16),
            jax.ShapeDtypeStruct((all_rows, units), BF16),
        ),
        in_specs=[smem, smem, vmem, vmem, vmem] + [hbm] * 5,
        out_specs=(vmem, vmem),
        scratch_shapes=[
            pltpu.VMEM(k_cache.shape, BF16),
            pltpu.VMEM(v_cache.shape, BF16),
            pltpu.VMEM((n_slots, units, cols), BF16),
            pltpu.VMEM((HD, HD), F32),
            pltpu.VMEM((HD, HD), F32),
            pltpu.VMEM((HD, HD), F32),
            pltpu.VMEM((2, 8, HD), F32),
            pltpu.VMEM((shards, rows, width), BF16),
            pltpu.VMEM((all_rows, width), F32),
            pltpu.VMEM((all_rows, cols), F32),
            pltpu.VMEM((n_kv, 2, all_rows, cols // 2), BF16),
            pltpu.VMEM((shards, all_rows, cols), BF16),
            pltpu.VMEM((shards, 1, cols), F32),
            pltpu.VMEM((all_rows, cols), BF16),
            pltpu.VMEM((all_rows, units), F32),
            pltpu.VMEM((all_rows, units), F32),
            dma((2,)),
            dma((n_slots,)),
            dma,
            dma,
            dma((shards - 1,)),
            dma((shards,)),
            dma((shards - 1,)),
            dma((shards,)),
            dma((2, n_kv - 1)),
            dma((2, n_kv)),
            dma((chips,)),
            dma((shards,)),
            dma((max(chips - 1, 1),)),
        ],
        compiler_params=pltpu.CompilerParams(
            collective_id=0, has_side_effects=True, vmem_limit_bytes=VMEM_BYTES - (1 << 20)
        ),
    )(
        page_table,
        seq_lens,
        queries,
        residual,
        gain,
        k_cache,
        v_cache,
        out_proj,
        gate,
        up,
    )


def solution(mesh):
    in_specs = (
        P("replica", "kvhead"),
        P(("replica", "ffn"), None, "kvhead"),
        P(("replica", "ffn"), None, "kvhead"),
        P("replica", "ffn"),
        P("replica"),
        P("kvhead", ("replica", "ffn")),
        P("kvhead", ("replica", "ffn")),
        P(("replica", "ffn")),
        P(("replica", "kvhead", "ffn"), None),
        P(("replica", "kvhead", "ffn"), None),
    )
    out_specs = (P("kvhead", ("replica", "ffn")), P(None, ("replica", "kvhead", "ffn")))
    sizes = (mesh.shape["replica"], mesh.shape["kvhead"], mesh.shape["ffn"])
    return jax.shard_map(
        functools.partial(per_device, sizes),
        mesh=mesh,
        in_specs=in_specs,
        out_specs=out_specs,
        check_vma=False,
    )
```

```python
import functools
import math

import jax
import jax.numpy as jnp
from jax import lax
from jax.experimental import pallas as pl
from jax.experimental.pallas import tpu as pltpu
from jax.sharding import PartitionSpec as P

D = 16384
HD = 128
GQ = 16


NEG_FILL = -1e30
NORM_EPS = 1e-05
MESH = pl.DeviceIdType.MESH
VMEM_BYTES = 67043328
F32 = jnp.float32
BF16 = jnp.bfloat16
NT = (((1,), (1,)), ((), ()))


def merged(part, axis, combine):
    gathered = jax.tree.map(lambda a: lax.all_gather(a, axis), part)

    def take(source):
        return jax.tree.map(lambda a: lax.dynamic_index_in_dim(a, source, 0, False), gathered)

    return lax.fori_loop(
        1, lax.axis_size(axis), lambda source, state: combine(state, take(source)), take(0)
    )


def join_parts(earlier, later):
    first_max, first_total, first_out = earlier
    second_max, second_total, second_out = later
    overall = jnp.maximum(first_max, second_max)
    first_factor = jnp.exp(first_max - overall)
    second_factor = jnp.exp(second_max - overall)
    joined_total = first_total * first_factor + second_total * second_factor
    joined_out = first_out * first_factor[..., None] + second_out * second_factor[..., None]
    return (overall, joined_total, joined_out)


def general_path(
    queries,
    k_cache,
    v_cache,
    page_table,
    seq_lens,
    out_proj,
    residual,
    norm_gain,
    gate_weight,
    up_weight,
):
    score_scale = 1.0 / math.sqrt(HD)
    row_count = queries.shape[0]
    local_heads = k_cache.shape[2] // HD
    span_len = page_table.shape[1] * k_cache.shape[1]
    key_rows = k_cache[page_table].reshape(row_count, span_len, local_heads, HD)
    value_rows = v_cache[page_table].reshape(row_count, span_len, local_heads, HD)
    query_heads = queries.reshape(row_count, local_heads, GQ, HD)
    scores = (
        jnp.einsum("rkgd,rskd->rkgs", query_heads, key_rows, preferred_element_type=jnp.float32)
        * score_scale
    )
    positions = lax.axis_index("ffn") * span_len + jnp.arange(span_len, dtype=jnp.int32)
    visible = (positions[None, :] < seq_lens[:, None])[:, None, None, :]
    block_max = jnp.max(jnp.where(visible, scores, NEG_FILL), axis=-1)
    weights = jnp.where(visible, jnp.exp(scores - block_max[..., None]), 0.0)
    block_total = jnp.sum(weights, axis=-1)
    block_out = jnp.einsum(
        "rkgs,rskd->rkgd",
        weights.astype(jnp.bfloat16),
        value_rows,
        preferred_element_type=jnp.float32,
    )
    overall, denominator, weighted = merged((block_max, block_total, block_out), "ffn", join_parts)
    contexts = (
        (weighted / denominator[..., None])
        .astype(jnp.bfloat16)
        .reshape(row_count, local_heads * GQ * HD)
    )
    partial_value = jnp.dot(
        lax.all_gather(contexts, "replica", axis=0, tiled=True),
        out_proj,
        preferred_element_type=jnp.float32,
    )
    own_count = residual.shape[0]
    own_first = lax.axis_index("kvhead") * own_count
    own_part = lax.dynamic_slice_in_dim(partial_value, own_first, own_count, 0) + residual.astype(
        jnp.float32
    )
    partial_value = lax.dynamic_update_slice_in_dim(partial_value, own_part, own_first, 0)
    gain_wide = norm_gain.astype(jnp.float32)
    summed = lax.psum(partial_value, "kvhead")
    post_all = summed.astype(jnp.bfloat16)
    post_attn = lax.dynamic_slice_in_dim(post_all, own_first, own_count, 0)
    widened = post_all.astype(jnp.float32)
    squares = lax.psum(jnp.sum(widened * widened, axis=1), ("replica", "ffn"))
    normed = (widened * lax.rsqrt(squares / D + NORM_EPS)[:, None] * gain_wide).astype(jnp.bfloat16)
    contract = (((1,), (1,)), ((), ()))
    shard_cols = lax.all_gather(normed, ("replica", "ffn"), axis=1, tiled=True)
    gate_sum = lax.dot_general(
        shard_cols, gate_weight, contract, preferred_element_type=jnp.float32
    )
    up_sum = lax.dot_general(shard_cols, up_weight, contract, preferred_element_type=jnp.float32)
    hidden = (jax.nn.silu(gate_sum) * up_sum).astype(jnp.bfloat16)
    return (post_attn, hidden)


def layer_kernel(
    sizes,
    page_ref,
    len_ref,
    query_ref,
    resid_ref,
    gain_ref,
    k_hbm,
    v_hbm,
    proj_hbm,
    gate_hbm,
    up_hbm,
    post_ref,
    hidden_ref,
    k_buf,
    v_buf,
    slots,
    q_heads,
    o_heads,
    stat_cols,
    stats,
    ctx_parts,
    ctx_wide,
    part,
    z_parts,
    blocks,
    gains,
    x_buf,
    gate_acc,
    up_acc,
    kv_sem,
    slot_sem,
    stat_send,
    stat_recv,
    ctx_send,
    ctx_recv,
    gain_send,
    gain_recv,
    z_send,
    z_recv,
    blk_send,
    blk_recv,
    fwd_send,
):
    n_rep, n_kv, n_ffn, n_slots, proj_rows = sizes
    replica = lax.axis_index("replica")
    kvhead = lax.axis_index("kvhead")
    ffn = lax.axis_index("ffn")
    rows, width = query_ref.shape
    heads = width // HD
    page_len = k_hbm.shape[1]
    kv_heads = k_hbm.shape[2] // HD
    pages = page_ref.shape[1]
    span = pages * page_len
    depth, cols = proj_hbm.shape
    all_rows = n_rep * rows
    own_rows = resid_ref.shape[0]
    n_chip = n_rep // 2
    chip, core = replica // 2, replica % 2

    def shard_of(rep, f):
        return rep * n_ffn + f

    me = shard_of(replica, ffn)

    def send(ref, index, sem_out, sem_in, target):
        return pltpu.make_async_remote_copy(
            src_ref=ref.at[index],
            dst_ref=ref.at[index],
            send_sem=sem_out,
            recv_sem=sem_in,
            device_id=target,
            device_id_type=MESH,
        )

    plane = []
    for a in range(n_chip):
        for c in range(2):
            for b in range(n_ffn):
                if (a, c, b) != (0, 0, 0):
                    rep = ((chip + a) % n_chip) * 2 + (core + c) % 2
                    plane.append((rep, (ffn + b) % n_ffn))
    lines = [(kvhead + k) % n_kv for k in range(1, n_kv)]

    k_copy = pltpu.make_async_copy(k_hbm, k_buf, kv_sem.at[0])
    v_copy = pltpu.make_async_copy(v_hbm, v_buf, kv_sem.at[1])
    k_copy.start()
    v_copy.start()
    proj_copies = []
    for i, first in enumerate(range(0, depth, proj_rows)):
        count = min(proj_rows, depth - first)
        copy = pltpu.make_async_copy(
            proj_hbm.at[pl.ds(first, count), :], slots.at[i, pl.ds(0, count), :], slot_sem.at[i]
        )
        proj_copies.append((copy, first, count))
    n_proj = len(proj_copies)

    direct = []
    for a in range(n_chip):
        for b in range(n_ffn):
            direct.append((a, b))
    direct.sort(key=lambda ab: (ab[0] + ab[1], ab[0]))
    order = [(0, 0, 0), (0, 0, 1)]
    order += [(a, b, 0) for a, b in direct[1:]] + [(a, b, 1) for a, b in direct[1:]]

    def place(a, b, c):
        rep = ((chip + a) % n_chip) * 2 + (core + c) % 2
        return rep, (ffn + b) % n_ffn

    weight_copies = []
    for step, where in enumerate(order):
        shard = shard_of(*place(*where))
        window = pl.ds(pl.multiple_of(shard * cols, cols), cols)
        for which, source in enumerate((gate_hbm, up_hbm)):
            slot = (n_proj + 2 * step + which) % n_slots
            weight_copies.append(
                pltpu.make_async_copy(source.at[:, window], slots.at[slot, pl.ds(0, source.shape[0]), :], slot_sem.at[slot])
            )
    early = n_slots - n_proj
    opening = min(4, early)

    barrier = pltpu.get_barrier_semaphore()
    for rep, f in plane:
        pl.semaphore_signal(
            barrier, inc=1, device_id={"replica": rep, "ffn": f}, device_id_type=MESH
        )
    for k in lines:
        pl.semaphore_signal(barrier, inc=1, device_id={"kvhead": k}, device_id_type=MESH)

    for h in range(heads):
        q_heads[pl.ds(h, rows, stride=heads), :] = query_ref[:, h * HD : (h + 1) * HD].astype(F32)
    gains[me] = gain_ref[...].astype(F32).reshape(1, cols)

    pl.semaphore_wait(barrier, len(plane) + len(lines))

    gain_copies = []
    for i, (rep, f) in enumerate(plane):
        copy = send(gains, me, gain_send.at[i], gain_recv.at[me], {"replica": rep, "ffn": f})
        copy.start()
        gain_copies.append(copy)

    scale = 1.0 / math.sqrt(HD)
    position = ffn * span + lax.broadcasted_iota(jnp.int32, (GQ, span), 1)
    lane = lax.broadcasted_iota(jnp.int32, (GQ, HD), 1)
    k_copy.wait()
    for copy, _, _ in proj_copies:
        copy.start()
    weights = []
    for r in range(rows):
        visible = position < len_ref[r]
        for g in range(kv_heads):
            keys = jnp.concatenate(
                [k_buf[page_ref[r, j], :, g * HD : (g + 1) * HD] for j in range(pages)], axis=0
            )
            first = (r * kv_heads + g) * GQ
            query = q_heads[first : first + GQ, :].astype(BF16)
            scores = lax.dot_general(query, keys, NT, preferred_element_type=F32) * scale
            top = jnp.max(jnp.where(visible, scores, NEG_FILL), axis=1, keepdims=True)
            weight = jnp.where(visible, jnp.exp(scores - top), 0.0)
            total = jnp.sum(weight, axis=1, keepdims=True)
            stat_cols[first : first + GQ, :] = jnp.where(
                lane < HD // 2,
                jnp.broadcast_to(top, (GQ, HD)),
                jnp.broadcast_to(total, (GQ, HD)),
            )
            weights.append(weight.astype(BF16))
    turned = stat_cols[...].T
    stats[0, 0:1, :] = turned[0:1, :]
    stats[0, 1:2, :] = turned[HD // 2 : HD // 2 + 1, :]
    stat_copy = pltpu.make_async_remote_copy(
        src_ref=stats.at[0],
        dst_ref=stats.at[1],
        send_sem=stat_send,
        recv_sem=stat_recv,
        device_id={"ffn": (ffn + 1) % n_ffn},
        device_id_type=MESH,
    )
    stat_copy.start()
    v_copy.wait()
    for r in range(rows):
        for g in range(kv_heads):
            values = jnp.concatenate(
                [v_buf[page_ref[r, j], :, g * HD : (g + 1) * HD] for j in range(pages)], axis=0
            )
            first = (r * kv_heads + g) * GQ
            o_heads[first : first + GQ, :] = jnp.dot(
                weights[r * kv_heads + g], values, preferred_element_type=F32
            )
    stat_copy.wait()
    own_top, own_total = stats[0, 0:1, :], stats[0, 1:2, :]
    far_top, far_total = stats[1, 0:1, :], stats[1, 1:2, :]
    overall = jnp.maximum(own_top, far_top)
    own_lift = jnp.exp(own_top - overall)
    far_lift = jnp.exp(far_top - overall)
    factor = own_lift / (own_lift * own_total + far_lift * far_total)
    o_heads[...] = o_heads[...] * jnp.broadcast_to(factor, (HD, HD)).T
    for h in range(heads):
        ctx_parts[me, :, h * HD : (h + 1) * HD] = o_heads[
            pl.ds(h, rows, stride=heads), :
        ].astype(BF16)
    ctx_copies = []
    for i, (rep, f) in enumerate(plane):
        copy = send(ctx_parts, me, ctx_send.at[i], ctx_recv.at[me], {"replica": rep, "ffn": f})
        copy.start()
        ctx_copies.append(copy)
    for copy in weight_copies[:opening]:
        copy.start()
    for rep, f in plane:
        shard = shard_of(rep, f)
        send(
            ctx_parts, shard, ctx_send.at[0], ctx_recv.at[shard], {"replica": rep, "ffn": f}
        ).wait_recv()
    for rep in range(n_rep):
        joined = ctx_parts[rep * n_ffn].astype(F32)
        for f in range(1, n_ffn):
            joined = joined + ctx_parts[rep * n_ffn + f].astype(F32)
        ctx_wide[rep * rows : (rep + 1) * rows, :] = joined

    resid = resid_ref[...].astype(F32)
    half = cols // 2
    z_copies = []
    for side in range(2):
        window = slice(side * half, (side + 1) * half)
        for i, (copy, first, count) in enumerate(proj_copies):
            if side == 0:
                copy.wait()
            term = jnp.dot(
                ctx_wide[:, first : first + count].astype(BF16),
                slots[i, 0:count, window],
                preferred_element_type=F32,
            )
            if i == 0:
                part[:, window] = term
            else:
                part[:, window] += term
        if side == 0:
            for copy in weight_copies[opening:early]:
                copy.start()
        else:
            for copy in weight_copies[early:]:
                copy.start()
        for k in range(n_kv):
            part[k * own_rows : (k + 1) * own_rows, window] += jnp.where(
                kvhead == k, resid[:, window], 0.0
            )
        z_parts[kvhead, side] = part[:, window].astype(BF16)
        for i, k in enumerate(lines):
            copy = send(
                z_parts,
                (kvhead, side),
                z_send.at[side, i],
                z_recv.at[side, kvhead],
                {"kvhead": k},
            )
            copy.start()
            z_copies.append(copy)
    gate_acc[...] = jnp.zeros_like(gate_acc)
    up_acc[...] = jnp.zeros_like(up_acc)
    for copy in gain_copies:
        copy.wait_send()
    for rep, f in plane:
        shard = shard_of(rep, f)
        send(
            gains, shard, gain_send.at[0], gain_recv.at[shard], {"replica": rep, "ffn": f}
        ).wait_recv()
    for copy in ctx_copies:
        copy.wait_send()
    for side in range(2):
        for k in lines:
            send(
                z_parts, (k, side), z_send.at[side, 0], z_recv.at[side, k], {"kvhead": k}
            ).wait_recv()
            part[:, side * half : (side + 1) * half] += z_parts[k, side].astype(F32)
    blocks[me] = part[...].astype(BF16)
    blk_copies = []
    for i, where in enumerate([(0, 0, 1)] + [(a, b, 0) for a, b in direct[1:]]):
        rep, f = place(*where)
        copy = send(blocks, me, blk_send.at[i], blk_recv.at[me], {"replica": rep, "ffn": f})
        copy.start()
        blk_copies.append(copy)
    own_post = jnp.zeros((own_rows, cols), F32)
    for k in range(n_kv):
        own_post = own_post + jnp.where(
            kvhead == k, part[k * own_rows : (k + 1) * own_rows, :], 0.0
        )
    post_ref[...] = own_post.astype(BF16)

    def arrive(where):
        rep, f = place(*where)
        shard = shard_of(rep, f)
        send(
            blocks, shard, blk_send.at[0], blk_recv.at[shard], {"replica": rep, "ffn": f}
        ).wait_recv()

    fwd_copies = []

    def pass_on(where):
        arrive(where)
        shard = shard_of(*place(*where))
        copy = send(
            blocks,
            shard,
            fwd_send.at[len(fwd_copies)],
            blk_recv.at[shard],
            {"replica": chip * 2 + (core + 1) % 2},
        )
        copy.start()
        fwd_copies.append(copy)

    squares = jnp.zeros((all_rows, 1), F32)
    pending = [(a, b, 0) for a, b in direct[1:]]
    piece = cols
    for step, where in enumerate(order):
        if step >= 1 and pending:
            pass_on(pending.pop(0))
            if pending:
                pass_on(pending.pop(0))
        if where[2] == 1:
            arrive(where)
        shard = shard_of(*place(*where))
        wide = blocks[shard].astype(F32)
        squares = squares + jnp.sum(wide * wide, axis=1, keepdims=True)
        x_buf[...] = (wide * gains[shard]).astype(BF16)
        weight_copies[2 * step].wait()
        weight_copies[2 * step + 1].wait()
        gate_slot = (n_proj + 2 * step) % n_slots
        up_slot = (n_proj + 2 * step + 1) % n_slots

        def accumulate(i, carry, gate_slot=gate_slot, up_slot=up_slot):
            window = pl.ds(pl.multiple_of(i * piece, piece), piece)
            part_x = x_buf[:, window]
            units = gate_acc.shape[1]
            gate_acc[...] += lax.dot_general(
                part_x, slots[gate_slot, 0:units, window], NT, preferred_element_type=F32
            )
            up_acc[...] += lax.dot_general(
                part_x, slots[up_slot, 0:units, window], NT, preferred_element_type=F32
            )
            return carry

        lax.fori_loop(0, cols // piece, accumulate, 0)
    inverse = lax.rsqrt(squares / D + NORM_EPS)
    gate = gate_acc[...] * inverse
    hidden_ref[...] = (gate / (1.0 + jnp.exp(-gate)) * (up_acc[...] * inverse)).astype(BF16)
    for copy in z_copies + blk_copies + fwd_copies:
        copy.wait_send()


def plan(n_rep, n_kv, n_ffn, shapes):
    queries, k_cache, v_cache, page_table, seq_lens, out_proj, residual, gain, gate, up = shapes
    depth, cols = out_proj
    units = gate[0]
    rows = queries[0]
    heads = queries[1] // HD
    if n_ffn != 2 or n_rep % 2 or units % 16 or cols % 256 or rows * heads != HD:
        return None
    if gate[1] != n_rep * n_ffn * cols or page_table[0] * page_table[1] != k_cache[0]:
        return None
    proj_rows = units // 256 * 256
    if proj_rows == 0:
        return None
    n_slots = 2 * n_rep * n_ffn
    n_proj = -(-depth // proj_rows)
    held = n_slots * units * cols * 2 + 4 * math.prod(k_cache)
    if n_proj > n_slots or held + (4 << 20) > VMEM_BYTES:
        return None
    return n_slots, proj_rows


def per_device(sizes, *args):
    (queries, k_cache, v_cache, page_table, seq_lens, out_proj, residual, gain, gate, up) = args
    n_rep, n_kv, n_ffn = sizes
    found = plan(n_rep, n_kv, n_ffn, [a.shape for a in args])
    if found is None:
        return general_path(*args)
    n_slots, proj_rows = found
    rows, width = queries.shape
    cols = out_proj.shape[1]
    units = gate.shape[0]
    all_rows = n_rep * rows
    shards = n_rep * n_ffn
    chips = shards // 2
    vmem = pl.BlockSpec(memory_space=pltpu.VMEM)
    smem = pl.BlockSpec(memory_space=pltpu.SMEM)
    hbm = pl.BlockSpec(memory_space=pl.ANY)
    dma = pltpu.SemaphoreType.DMA
    return pl.pallas_call(
        functools.partial(layer_kernel, (n_rep, n_kv, n_ffn, n_slots, proj_rows)),
        out_shape=(
            jax.ShapeDtypeStruct(residual.shape, BF16),
            jax.ShapeDtypeStruct((all_rows, units), BF16),
        ),
        in_specs=[smem, smem, vmem, vmem, vmem] + [hbm] * 5,
        out_specs=(vmem, vmem),
        scratch_shapes=[
            pltpu.VMEM(k_cache.shape, BF16),
            pltpu.VMEM(v_cache.shape, BF16),
            pltpu.VMEM((n_slots, units, cols), BF16),
            pltpu.VMEM((HD, HD), F32),
            pltpu.VMEM((HD, HD), F32),
            pltpu.VMEM((HD, HD), F32),
            pltpu.VMEM((2, 8, HD), F32),
            pltpu.VMEM((shards, rows, width), BF16),
            pltpu.VMEM((all_rows, width), F32),
            pltpu.VMEM((all_rows, cols), F32),
            pltpu.VMEM((n_kv, 2, all_rows, cols // 2), BF16),
            pltpu.VMEM((shards, all_rows, cols), BF16),
            pltpu.VMEM((shards, 1, cols), F32),
            pltpu.VMEM((all_rows, cols), BF16),
            pltpu.VMEM((all_rows, units), F32),
            pltpu.VMEM((all_rows, units), F32),
            dma((2,)),
            dma((n_slots,)),
            dma,
            dma,
            dma((shards - 1,)),
            dma((shards,)),
            dma((shards - 1,)),
            dma((shards,)),
            dma((2, n_kv - 1)),
            dma((2, n_kv)),
            dma((chips,)),
            dma((shards,)),
            dma((max(chips - 1, 1),)),
        ],
        compiler_params=pltpu.CompilerParams(
            collective_id=0, has_side_effects=True, vmem_limit_bytes=VMEM_BYTES - (1 << 20)
        ),
    )(
        page_table,
        seq_lens,
        queries,
        residual,
        gain,
        k_cache,
        v_cache,
        out_proj,
        gate,
        up,
    )


def solution(mesh):
    in_specs = (
        P("replica", "kvhead"),
        P(("replica", "ffn"), None, "kvhead"),
        P(("replica", "ffn"), None, "kvhead"),
        P("replica", "ffn"),
        P("replica"),
        P("kvhead", ("replica", "ffn")),
        P("kvhead", ("replica", "ffn")),
        P(("replica", "ffn")),
        P(("replica", "kvhead", "ffn"), None),
        P(("replica", "kvhead", "ffn"), None),
    )
    out_specs = (P("kvhead", ("replica", "ffn")), P(None, ("replica", "kvhead", "ffn")))
    sizes = (mesh.shape["replica"], mesh.shape["kvhead"], mesh.shape["ffn"])
    return jax.shard_map(
        functools.partial(per_device, sizes),
        mesh=mesh,
        in_specs=in_specs,
        out_specs=out_specs,
        check_vma=False,
    )
```
